32 devices in a mesh: row: 4 (over x, core), col: 8 (over z, y).
Axes of the slice: x: 2, y: 2, z: 4, core: 2. Of those that a mesh axis runs over, the one named last changes fastest.
Arguments:
- tokens: bfloat16 [128, 12288], P('col', 'row'), may hold values from -6 to 6
- w_in: bfloat16 [12288, 24576], P('row', 'col'), may hold values from -0.078125 to 0.078125
- w_out: bfloat16 [24576, 12288], P('col', 'row'), may hold values from -0.0546875 to 0.0546875
- mask_in: int32 [96, 192], P('row', 'col'), may hold values 0 or 1
- mask_out: int32 [192, 96], P('col', 'row'), may hold values 0 or 1
- out_grad: bfloat16 [128, 12288], P('col', 'row'), may hold values from -1.5 to 1.5
Outputs:
- mixed: bfloat16 [128, 12288], P('col', 'row')
- tokens_grad: bfloat16 [128, 12288], P('col', 'row')
- w_in_grad: bfloat16 [12288, 24576], P('row', 'col')
- w_out_grad: bfloat16 [24576, 12288], P('col', 'row')
The draws below stay inside these ranges and needn't reach their ends.
Inputs may be any that keep to these rules, and one draw needn't show every extreme that they name: `mask_in`: one flag per block. `mask_out`: one flag per block.
All inputs are finite; a program needn't handle non-finite values.
Results may differ from the reference program's by a relative error of at most 0.0049.
Values may be sent and summed in bfloat16 or wider, within the bound.
A program may use at most 192 MiB of HBM per device.

```python
import jax
import jax.numpy as jnp

D = 12288
FF = 24576
BLK = 128
TOKENS = 128


def set_ends(entries, own_key, least, high):
    longest = entries.shape.index(max(entries.shape))
    spots = []
    for shift in (0, 1):
        where = [jax.random.randint(jax.random.fold_in(own_key, axis), (), 0, length) for axis, length in enumerate(entries.shape)]
        where[longest] = (where[longest] + shift) % entries.shape[longest]
        spots.append(tuple(where))
    return entries.at[spots[0]].set(least).at[spots[1]].set(high)


def steps_of(own_key, shape, shards, least, top_value):
    factor_of, own = 1.0, jax.random.fold_in(own_key, 6)
    for dim, parts in shards:
        steps = jnp.exp(jax.random.uniform(jax.random.fold_in(own, dim), (parts,), jnp.float32, least / len(shards), top_value / len(shards)))
        factor_of = factor_of * jnp.repeat(steps, shape[dim] // parts).reshape([-1 if axis == dim else 1 for axis in range(len(shape))])
    return factor_of


def centred(key, extent, spread, reach, pieces=(), held_as=jnp.bfloat16):
    drawn = jax.random.normal(key, extent, jnp.float32) * spread
    if len(pieces) > 0:
        drawn = steps_of(key, extent, pieces, -0.22, 0.18) * drawn
    return jnp.clip(drawn, min=-reach, max=reach).astype(held_as)


def setup_inputs(seed: int = 0) -> dict:
    seeds = jax.random.split(jax.random.key(seed), 7)
    return {
        "tokens": centred(seeds[0], (TOKENS, D), 1.0, 6.0, ((0, 8), (1, 4))),
        "w_in": centred(seeds[1], (D, FF), (D // 2) ** -0.5, 0.078125, ((0, 4), (1, 8))),
        "w_out": centred(seeds[2], (FF, D), (FF // 2) ** -0.5, 0.0546875, ((0, 8), (1, 4))),
        "mask_in": set_ends((jax.random.randint(seeds[3], (D // BLK, FF // BLK), 0, 2) < 1).astype(jnp.int32), jax.random.fold_in(seeds[3], 1), 0, 1),
        "mask_out": set_ends((jax.random.randint(seeds[4], (FF // BLK, D // BLK), 0, 2) < 1).astype(jnp.int32), jax.random.fold_in(seeds[4], 1), 0, 1),
        "out_grad": centred(seeds[5], (TOKENS, D), 0.25, 1.5, ((0, 8), (1, 4))),
    }


def apply_mask(weight, mask, blk):
    rows, cols = weight.shape
    shaped = weight.reshape(rows // blk, blk, cols // blk, blk)
    return (shaped * mask[:, None, :, None].astype(weight.dtype)).reshape(rows, cols)

def gelu_tanh(value):
    return jax.nn.gelu(value, approximate=True)

def reference(tokens, w_in, w_out, mask_in, mask_out, out_grad):
    win = apply_mask(w_in, mask_in, BLK)
    wout = apply_mask(w_out, mask_out, BLK)
    hidden = jnp.dot(tokens, win, preferred_element_type=jnp.float32)
    act = gelu_tanh(hidden).astype(jnp.bfloat16)
    mixed = jnp.dot(act, wout, preferred_element_type=jnp.float32).astype(jnp.bfloat16)
    act_grad = jnp.dot(out_grad, wout.T, preferred_element_type=jnp.float32)
    unused, pull = jax.vjp(gelu_tanh, hidden)
    hid_grad = pull(act_grad)[0].astype(jnp.bfloat16)
    w_out_grad = apply_mask(jnp.dot(act.T, out_grad, preferred_element_type=jnp.float32), mask_out, BLK).astype(jnp.bfloat16)
    tokens_grad = jnp.dot(hid_grad, win.T, preferred_element_type=jnp.float32).astype(jnp.bfloat16)
    w_in_grad = apply_mask(jnp.dot(tokens.T, hid_grad, preferred_element_type=jnp.float32), mask_in, BLK).astype(jnp.bfloat16)
    return (mixed, tokens_grad, w_in_grad, w_out_grad)
```

```python
import functools
import math

import jax
import jax.numpy as jnp
from jax import lax
from jax.experimental import pallas as pl
from jax.experimental.pallas import tpu as pltpu
from jax.sharding import PartitionSpec as P

BLK = 128
SUB = 16
MESH = pl.DeviceIdType.MESH
VMEM = pl.BlockSpec(memory_space=pltpu.VMEM)
DMA = pltpu.SemaphoreType.DMA
GELU_A, GELU_B = 0.7978845608028654, 0.044715


def remote(src, dst, send, recv, axis, device):
    return pltpu.make_async_remote_copy(
        src_ref=src, dst_ref=dst, send_sem=send, recv_sem=recv,
        device_id={axis: device}, device_id_type=MESH,
    )


def greet(axis, peers):
    barrier = pltpu.get_barrier_semaphore()
    for peer in peers:
        pl.semaphore_signal(barrier, inc=1, device_id={axis: peer}, device_id_type=MESH)
    pl.semaphore_wait(barrier, len(peers))


def gather_kernel(far, near, *refs):
    srcs, dsts, (zs, zr, ys, yr, own) = refs[:2], refs[2:4], refs[4:]
    me = lax.axis_index("col")
    z, y = me // near, lax.rem(me, near)
    along_z = [lax.rem(z + d, far) * near + y for d in range(1, far)]
    along_y = [z * near + lax.rem(y + e, near) for e in range(1, near)]
    greet("col", along_z + along_y)
    sent = []
    for a in range(2):
        for e, peer in enumerate(along_y):
            sent.append(remote(srcs[a], dsts[a].at[me], ys.at[a, 0, e], yr.at[a, 0, e], "col", peer))
            sent[-1].start()
        for d, peer in enumerate(along_z):
            sent.append(remote(srcs[a], dsts[a].at[me], zs.at[a, d], zr.at[a, d], "col", peer))
            sent[-1].start()
    kept = [pltpu.make_async_copy(srcs[a], dsts[a].at[me], own.at[a]) for a in range(2)]
    for copy in kept:
        copy.start()
    for a in range(2):
        for d in range(far - 1):
            block = lax.rem(z + far - d - 1, far) * near + y
            slot = dsts[a].at[block]
            remote(srcs[a], slot, zs.at[a, d], zr.at[a, d], "col", along_z[d]).wait_recv()
            for e, peer in enumerate(along_y):
                sent.append(remote(slot, slot, ys.at[a, d + 1, e], yr.at[a, d + 1, e], "col", peer))
                sent[-1].start()
    for a in range(2):
        for d in range(far):
            for e in range(near - 1):
                block = lax.rem(z + far - d, far) * near + lax.rem(y + near - e - 1, near)
                slot = dsts[a].at[block]
                remote(slot, slot, ys.at[a, d, e], yr.at[a, d, e], "col", along_y[e]).wait_recv()
    for copy in sent:
        copy.wait_send()
    for copy in kept:
        copy.wait()


def gather(far, near, first, second):
    out = jax.ShapeDtypeStruct((far * near,) + first.shape, first.dtype)
    gathered = pl.pallas_call(
        functools.partial(gather_kernel, far, near),
        out_shape=(out, out),
        in_specs=[VMEM, VMEM],
        out_specs=(VMEM, VMEM),
        scratch_shapes=[
            DMA((2, far - 1)), DMA((2, far - 1)),
            DMA((2, far, near - 1)), DMA((2, far, near - 1)), DMA((2,)),
        ],
        compiler_params=pltpu.CompilerParams(collective_id=0, has_side_effects=True),
        name="gather_col",
    )(first, second)
    return [each.reshape(-1, first.shape[1]) for each in gathered]


def gelu_parts(value):
    square = value * value
    tanh = jnp.tanh(GELU_A * (value + GELU_B * (square * value)))
    half = 0.5 * (1.0 + tanh)
    slope = half + 0.5 * value * (1.0 - tanh * tanh) * (GELU_A * (1.0 + (3.0 * GELU_B) * square))
    return value * half, slope


def row_kernel(chips, cores, *refs):
    parts, outs = refs[:2], refs[2:4]
    pair, sums, landed, slope, ps, pr, xs, xr, gs, gr, fs, fr = refs[4:]
    me = lax.axis_index("row")
    x, k = me // cores, lax.rem(me, cores)
    partner = x * cores + (1 - k)
    across = [lax.rem(x + d, chips) for d in range(1, chips)]
    peers = [c * cores + k for c in across]
    greet("row", [partner] + peers)
    sent = []
    for a in range(2):
        for d, c in enumerate(across + [x]):
            sent.append(remote(parts[a].at[c, 1 - k], pair.at[a, c], ps.at[a, d], pr.at[a, d], "row", partner))
            sent[-1].start()
    for a in range(2):
        for d, c in enumerate(across):
            remote(parts[a].at[c, 1 - k], pair.at[a, c], ps.at[a, d], pr.at[a, d], "row", partner).wait_recv()
            sums[a, d] = (parts[a][c, k] + pair[a, c]).astype(sums.dtype)
            sent.append(remote(sums.at[a, d], landed.at[a, d], xs.at[a, d], xr.at[a, d], "row", peers[d]))
            sent[-1].start()
    for a in range(2):
        last = chips - 1
        remote(parts[a].at[x, 1 - k], pair.at[a, x], ps.at[a, last], pr.at[a, last], "row", partner).wait_recv()
        total = parts[a][x, k] + pair[a, x]
        for d in range(chips - 1):
            remote(sums.at[a, d], landed.at[a, d], xs.at[a, d], xr.at[a, d], "row", peers[d]).wait_recv()
            total = total + landed[a, d].astype(jnp.float32)
        if a == 0:
            act, rate = gelu_parts(total)
            slope[...] = rate
            outs[a][me] = act.astype(outs[a].dtype)
        else:
            outs[a][me] = (total * slope[...]).astype(outs[a].dtype)
        mine = outs[a].at[me]
        for d, peer in enumerate(peers):
            sent.append(remote(mine, mine, gs.at[a, d], gr.at[a, d], "row", peer))
            sent[-1].start()
        sent.append(remote(mine, mine, fs.at[a, chips - 1], fr.at[a, chips - 1], "row", partner))
        sent[-1].start()
    for a in range(2):
        for d in range(chips - 1):
            slot = outs[a].at[lax.rem(x + chips - d - 1, chips) * cores + k]
            remote(slot, slot, gs.at[a, d], gr.at[a, d], "row", peers[d]).wait_recv()
            sent.append(remote(slot, slot, fs.at[a, d], fr.at[a, d], "row", partner))
            sent[-1].start()
    for a in range(2):
        for d in range(chips):
            slot = outs[a].at[lax.rem(x + chips - lax.rem(d + 1, chips), chips) * cores + (1 - k)]
            remote(slot, slot, fs.at[a, d], fr.at[a, d], "row", partner).wait_recv()
    for copy in sent:
        copy.wait_send()


def row_exchange(chips, cores, first, second):
    tokens, width = first.shape
    share = tokens // (chips * cores)
    out = jax.ShapeDtypeStruct((chips * cores, share, width), jnp.bfloat16)
    shaped = (chips, cores, share, width)
    gathered = pl.pallas_call(
        functools.partial(row_kernel, chips, cores),
        out_shape=(out, out),
        in_specs=[VMEM, VMEM],
        out_specs=(VMEM, VMEM),
        scratch_shapes=[
            pltpu.VMEM((2, chips, share, width), jnp.float32),
            pltpu.VMEM((2, chips - 1, share, width), jnp.bfloat16),
            pltpu.VMEM((2, chips - 1, share, width), jnp.bfloat16),
            pltpu.VMEM((share, width), jnp.float32),
            DMA((2, chips)), DMA((2, chips)),
            DMA((2, chips - 1)), DMA((2, chips - 1)),
            DMA((2, chips - 1)), DMA((2, chips - 1)),
            DMA((2, chips)), DMA((2, chips)),
        ],
        compiler_params=pltpu.CompilerParams(collective_id=1, has_side_effects=True),
        name="row_exchange",
    )(first.reshape(shaped), second.reshape(shaped))
    return [each.reshape(tokens, width) for each in gathered]


def column_kernel(far, near, pieces, *refs):
    wide, short, outs = refs[:2], refs[2:4], refs[4:6]
    across, sums, landed, ys, yr, zs, zr = refs[6:]
    me = lax.axis_index("col")
    z, y = me // near, lax.rem(me, near)
    rows_y = [lax.rem(y + e, near) for e in range(1, near)]
    rows_z = [lax.rem(z + d, far) for d in range(1, far)]
    peers_y = [z * near + e for e in rows_y]
    peers_z = [d * near + y for d in rows_z]
    greet("col", peers_y + peers_z)
    width = outs[0].shape[-1] // pieces
    steps = [(a, p) for a in range(2) for p in range(pieces)]
    cut = lambda p: pl.ds(p * width, width)
    sent = []

    def over_y(i, e):
        a, p = steps[i]
        return remote(short[a].at[:, rows_y[e], :, cut(p)], across.at[i, e], ys.at[i, e], yr.at[i, e], "col", peers_y[e])

    def over_z(i, d):
        return remote(sums.at[i, d], landed.at[i, d], zs.at[i, d], zr.at[i, d], "col", peers_z[d])

    def pair_sum(i, row):
        a, p = steps[i]
        total = wide[a][row, y, :, cut(p)]
        for e in range(near - 1):
            total = total + across[i, e, row].astype(jnp.float32)
        return total

    for i in range(len(steps)):
        for e in range(near - 1):
            sent.append(over_y(i, e))
            sent[-1].start()
    for i in range(len(steps)):
        for e in range(near - 1):
            over_y(i, e).wait_recv()
        for d in range(far - 1):
            sums[i, d] = pair_sum(i, rows_z[d]).astype(sums.dtype)
            sent.append(over_z(i, d))
            sent[-1].start()
    for i, (a, p) in enumerate(steps):
        total = pair_sum(i, z)
        for d in range(far - 1):
            over_z(i, d).wait_recv()
            total = total + landed[i, d].astype(jnp.float32)
        outs[a][:, cut(p)] = total.astype(outs[a].dtype)
    for copy in sent:
        copy.wait_send()


def column_sums(far, near, wide, short):
    tokens, width = wide[0].shape
    share = tokens // (far * near)
    pieces = 2
    cols = width // pieces
    out = jax.ShapeDtypeStruct((share, width), jnp.bfloat16)
    shaped = (far, near, share, width)
    count = 2 * pieces
    return pl.pallas_call(
        functools.partial(column_kernel, far, near, pieces),
        out_shape=(out, out),
        in_specs=[VMEM] * 4,
        out_specs=(VMEM, VMEM),
        scratch_shapes=[
            pltpu.VMEM((count, near - 1, far, share, cols), jnp.bfloat16),
            pltpu.VMEM((count, far - 1, share, cols), jnp.bfloat16),
            pltpu.VMEM((count, far - 1, share, cols), jnp.bfloat16),
            DMA((count, near - 1)), DMA((count, near - 1)),
            DMA((count, far - 1)), DMA((count, far - 1)),
        ],
        compiler_params=pltpu.CompilerParams(collective_id=2, has_side_effects=True),
        name="column_sums",
    )(*[each.reshape(shaped) for each in (*wide, *short)])


def masked(weight, flags):
    rows, cols = weight.shape
    shaped = weight.reshape(rows // BLK, BLK // SUB, SUB, cols)
    return (shaped * flags.reshape(rows // BLK, 1, SUB, cols)).reshape(rows, cols)


def products_kernel(left_ref, right_ref, down_ref, down_flags, up_ref, up_flags, *outs):
    ahead = jnp.dot(left_ref[...], masked(down_ref[...], down_flags[...]), preferred_element_type=jnp.float32)
    back = lax.dot_general(
        right_ref[...], masked(up_ref[...], up_flags[...]),
        (((1,), (1,)), ((), ())), preferred_element_type=jnp.float32,
    )
    outs[0][...], outs[1][...] = ahead, back
    if len(outs) > 2:
        outs[2][...], outs[3][...] = ahead.astype(outs[2].dtype), back.astype(outs[3].dtype)


def products(left, right, down, down_flags, up, up_flags, short):
    tokens, depth = left.shape
    width = down.shape[1]
    tile = 2 * BLK if width % (2 * BLK) == 0 else BLK
    per = tile // BLK * SUB
    whole = lambda each: pl.BlockSpec(each.shape, lambda i: (0, 0))
    kinds = [jnp.float32] * 2 + [jnp.bfloat16] * (2 if short else 0)
    return pl.pallas_call(
        products_kernel,
        grid=(width // tile,),
        out_shape=[jax.ShapeDtypeStruct((tokens, width), kind) for kind in kinds],
        in_specs=[
            whole(left), whole(right),
            pl.BlockSpec((depth, tile), lambda i: (0, i)),
            pl.BlockSpec((depth // BLK * SUB, tile), lambda i: (0, i)),
            pl.BlockSpec((tile, depth), lambda i: (i, 0)),
            pl.BlockSpec((per, depth), lambda i: (i, 0)),
        ],
        out_specs=[pl.BlockSpec((tokens, tile), lambda i: (0, i))] * len(kinds),
        name="products",
    )(left, right, down, down_flags, up, up_flags)


def outer_kernel(tokens_ref, hid_ref, in_flags, act_ref, grad_ref, out_flags, in_ref, out_ref):
    def one(left, right, flags, out):
        full = lax.dot_general(left, right, (((0,), (0,)), ((), ())), preferred_element_type=jnp.float32)
        out[...] = masked(full.astype(out.dtype), flags)

    one(tokens_ref[...], hid_ref[...], in_flags[...], in_ref)
    one(act_ref[...], grad_ref[...], out_flags[...], out_ref)


def outers(tokens, hid, in_flags, act, grad, out_flags):
    count, depth = tokens.shape
    width = hid.shape[1]
    steps = math.gcd(depth // BLK, width // BLK)
    steps = steps // 2 if steps % 2 == 0 else steps
    down, up = depth // steps, width // steps
    whole = lambda each: pl.BlockSpec(each.shape, lambda i: (0, 0))
    return pl.pallas_call(
        outer_kernel,
        grid=(steps,),
        out_shape=[
            jax.ShapeDtypeStruct((depth, width), jnp.bfloat16),
            jax.ShapeDtypeStruct((width, depth), jnp.bfloat16),
        ],
        in_specs=[
            pl.BlockSpec((count, down), lambda i: (0, i)), whole(hid),
            pl.BlockSpec((down // BLK * SUB, width), lambda i: (i, 0)),
            pl.BlockSpec((count, up), lambda i: (0, i)), whole(grad),
            pl.BlockSpec((up // BLK * SUB, depth), lambda i: (i, 0)),
        ],
        out_specs=[
            pl.BlockSpec((down, width), lambda i: (i, 0)),
            pl.BlockSpec((up, depth), lambda i: (i, 0)),
        ],
        name="outers",
    )(tokens, hid, in_flags, act, grad, out_flags)


def spread(mask):
    rows, cols = mask.shape
    flags = mask.astype(jnp.bfloat16)[:, None, :, None]
    return jnp.broadcast_to(flags, (rows, SUB, cols, BLK)).reshape(rows * SUB, cols * BLK)


def local(far, near, chips, cores, tokens, w_in, w_out, mask_in, mask_out, out_grad):
    in_flags, out_flags = spread(mask_in), spread(mask_out)
    gathered, grad_rows = gather(far, near, tokens, out_grad)
    hidden, act_grad = products(gathered, grad_rows, w_in, in_flags, w_out, out_flags, False)
    act, hid = row_exchange(chips, cores, hidden, act_grad)
    sums = products(act, hid, w_out, out_flags, w_in, in_flags, True)
    mixed, tokens_grad = column_sums(far, near, sums[:2], sums[2:])
    w_in_grad, w_out_grad = outers(gathered, hid, in_flags, act, grad_rows, out_flags)
    return (mixed, tokens_grad, w_in_grad, w_out_grad)


def solution(mesh):
    columns, rows = mesh.shape["col"], mesh.shape["row"]
    near = 2 ** (int(math.log2(columns)) // 2)
    return jax.shard_map(
        functools.partial(local, columns // near, near, rows // 2, 2),
        mesh=mesh,
        in_specs=(
            P("col", "row"),
            P("row", "col"),
            P("col", "row"),
            P("row", "col"),
            P("col", "row"),
            P("col", "row"),
        ),
        out_specs=(P("col", "row"), P("col", "row"), P("row", "col"), P("col", "row")),
        check_vma=False,
    )
```

```python
import functools
import math

import jax
import jax.numpy as jnp
from jax import lax
from jax.experimental import pallas as pl
from jax.experimental.pallas import tpu as pltpu
from jax.sharding import PartitionSpec as P

BLK = 128
SUB = 16
MESH = pl.DeviceIdType.MESH
VMEM = pl.BlockSpec(memory_space=pltpu.VMEM)
DMA = pltpu.SemaphoreType.DMA
GELU_A, GELU_B = 0.7978845608028654, 0.044715


def remote(src, dst, send, recv, axis, device):
    return pltpu.make_async_remote_copy(
        src_ref=src, dst_ref=dst, send_sem=send, recv_sem=recv,
        device_id={axis: device}, device_id_type=MESH,
    )


def greet(axis, peers):
    barrier = pltpu.get_barrier_semaphore()
    for peer in peers:
        pl.semaphore_signal(barrier, inc=1, device_id={axis: peer}, device_id_type=MESH)
    pl.semaphore_wait(barrier, len(peers))


def gather_kernel(far, near, *refs):
    srcs, masks, dsts, flags, (zs, zr, ys, yr, own) = refs[:2], refs[2:4], refs[4:6], refs[6:8], refs[8:]
    me = lax.axis_index("col")
    z, y = me // near, lax.rem(me, near)
    along_z = [lax.rem(z + d, far) * near + y for d in range(1, far)]
    along_y = [z * near + lax.rem(y + e, near) for e in range(1, near)]
    greet("col", along_z + along_y)
    sent = []
    for a in range(2):
        for e, peer in enumerate(along_y):
            sent.append(remote(srcs[a], dsts[a].at[me], ys.at[a, 0, e], yr.at[a, 0, e], "col", peer))
            sent[-1].start()
        for d, peer in enumerate(along_z):
            sent.append(remote(srcs[a], dsts[a].at[me], zs.at[a, d], zr.at[a, d], "col", peer))
            sent[-1].start()
    kept = [pltpu.make_async_copy(srcs[a], dsts[a].at[me], own.at[a]) for a in range(2)]
    for copy in kept:
        copy.start()
    for a in range(2):
        flags[a][...] = spread(masks[a][...])
    for a in range(2):
        for d in range(far - 1):
            block = lax.rem(z + far - d - 1, far) * near + y
            slot = dsts[a].at[block]
            remote(srcs[a], slot, zs.at[a, d], zr.at[a, d], "col", along_z[d]).wait_recv()
            for e, peer in enumerate(along_y):
                sent.append(remote(slot, slot, ys.at[a, d + 1, e], yr.at[a, d + 1, e], "col", peer))
                sent[-1].start()
    for a in range(2):
        for d in range(far):
            for e in range(near - 1):
                block = lax.rem(z + far - d, far) * near + lax.rem(y + near - e - 1, near)
                slot = dsts[a].at[block]
                remote(slot, slot, ys.at[a, d, e], yr.at[a, d, e], "col", along_y[e]).wait_recv()
    for copy in sent:
        copy.wait_send()
    for copy in kept:
        copy.wait()


def gather(far, near, first, second, masks):
    out = jax.ShapeDtypeStruct((far * near,) + first.shape, first.dtype)
    spreads = tuple(
        jax.ShapeDtypeStruct((each.shape[0] * SUB, each.shape[1] * BLK), jnp.bfloat16) for each in masks
    )
    *gathered, in_flags, out_flags = pl.pallas_call(
        functools.partial(gather_kernel, far, near),
        out_shape=(out, out) + spreads,
        in_specs=[VMEM] * 4,
        out_specs=(VMEM,) * 4,
        scratch_shapes=[
            DMA((2, far - 1)), DMA((2, far - 1)),
            DMA((2, far, near - 1)), DMA((2, far, near - 1)), DMA((2,)),
        ],
        compiler_params=pltpu.CompilerParams(collective_id=0, has_side_effects=True),
        name="gather_col",
    )(first, second, *masks)
    return [each.reshape(-1, first.shape[1]) for each in gathered] + [in_flags, out_flags]


def spread(mask):
    rows, cols = mask.shape

    def repeats(shape, dim, size):
        apart = lax.broadcasted_iota(jnp.int32, shape, dim) - size * lax.broadcasted_iota(jnp.int32, shape, 1 - dim)
        return jnp.where((apart >= 0) & (apart < size), 1.0, 0.0).astype(jnp.bfloat16)

    flags = mask.astype(jnp.float32).astype(jnp.bfloat16)
    tall = jnp.dot(repeats((rows * SUB, rows), 0, SUB), flags, preferred_element_type=jnp.float32)
    wide = jnp.dot(tall.astype(jnp.bfloat16), repeats((cols, cols * BLK), 1, BLK), preferred_element_type=jnp.float32)
    return wide.astype(jnp.bfloat16)


def masked(weight, flags):
    rows, cols = weight.shape
    shaped = weight.reshape(rows // BLK, BLK // SUB, SUB, cols)
    return (shaped * flags.reshape(rows // BLK, 1, SUB, cols)).reshape(rows, cols)


def tiling(width):
    tile = 2 * BLK if width % (2 * BLK) == 0 else BLK
    tiles = width // tile
    pieces = next(count for count in (4, 3, 2, 1) if tiles % count == 0)
    return tile, tiles, pieces


def stream_shapes(depth, tile):
    return [
        pltpu.VMEM((2, depth, tile), jnp.bfloat16), pltpu.VMEM((2, depth // BLK * SUB, tile), jnp.bfloat16),
        pltpu.VMEM((2, tile, depth), jnp.bfloat16), pltpu.VMEM((2, tile // BLK * SUB, depth), jnp.bfloat16),
        DMA((4, 2)),
    ]


def streamed(tile, tiles, left, right, sources, buffers):
    *slots, arrived = buffers
    rows = tile // BLK * SUB

    def copies(t):
        slot = lax.rem(t, 2)
        across = pl.ds(pl.multiple_of(t * tile, tile), tile)
        down = pl.ds(pl.multiple_of(t * rows, rows), rows)
        views = [sources[0].at[:, across], sources[1].at[:, across], sources[2].at[across, :], sources[3].at[down, :]]
        return [pltpu.make_async_copy(view, slots[n].at[slot], arrived.at[n, slot]) for n, view in enumerate(views)]

    def first():
        for copy in copies(0):
            copy.start()

    def pair(t):
        for copy in copies(t):
            copy.wait()

        @pl.when(t + 1 < tiles)
        def _():
            for copy in copies(t + 1):
                copy.start()

        slot = lax.rem(t, 2)
        ahead = jnp.dot(left[...], masked(slots[0][slot], slots[1][slot]), preferred_element_type=jnp.float32)
        back = lax.dot_general(
            right[...], masked(slots[2][slot], slots[3][slot]),
            (((1,), (1,)), ((), ())), preferred_element_type=jnp.float32,
        )
        return ahead, back

    return first, pair


def gelu_parts(value):
    square = value * value
    tanh = jnp.tanh(GELU_A * (value + GELU_B * (square * value)))
    half = 0.5 * (1.0 + tanh)
    slope = half + 0.5 * value * (1.0 - tanh * tanh) * (GELU_A * (1.0 + (3.0 * GELU_B) * square))
    return value * half, slope


def row_kernel(chips, cores, tile, tiles, pieces, left, right, *refs):
    sources, outs, refs = refs[:4], refs[4:6], refs[6:]
    buffers, refs = refs[:5], refs[5:]
    parts, pair, sums, landed, ps, pr, xs, xr, gs, gr, fs, fr = refs
    me = lax.axis_index("row")
    x, k = me // cores, lax.rem(me, cores)
    partner = x * cores + (1 - k)
    across = [lax.rem(x + d, chips) for d in range(1, chips)]
    peers = [c * cores + k for c in across]
    first, multiply = streamed(tile, tiles, left, right, sources, buffers)
    first()
    greet("row", [partner] + peers)
    per = tiles // pieces
    cols = per * tile
    shaped = parts.shape[2:5]
    sent = []

    def push(copy):
        copy.start()
        sent.append(copy)

    def to_partner(a, p):
        return remote(parts.at[a, p, :, 1 - k], pair.at[a, p], ps.at[a, p], pr.at[a, p], "row", partner)

    def to_chip(a, p, d):
        return remote(sums.at[a, p, d], landed.at[a, p, d], xs.at[a, p, d], xr.at[a, p, d], "row", peers[d])

    def share(a, p, owner):
        return outs[a].at[owner, :, pl.ds(p * cols, cols)]

    def give_chip(a, p, d, owner):
        return remote(share(a, p, owner), share(a, p, owner), gs.at[a, p, d], gr.at[a, p, d], "row", peers[d])

    def give_partner(a, p, d, owner):
        return remote(share(a, p, owner), share(a, p, owner), fs.at[a, p, d], fr.at[a, p, d], "row", partner)

    def compute(p):
        def step(j, carry):
            spot = pl.ds(pl.multiple_of(j * tile, tile), tile)
            for a, value in enumerate(multiply(p * per + j)):
                parts[a, p, :, :, :, spot] = value.reshape(*shaped, tile)
            return carry

        lax.fori_loop(0, per, step, 0)
        for a in range(2):
            push(to_partner(a, p))

    def reduce_pair(p):
        for a in range(2):
            to_partner(a, p).wait_recv()
            for d, c in enumerate(across):
                sums[a, p, d] = (parts[a, p, c, k] + pair[a, p, c]).astype(sums.dtype)
                push(to_chip(a, p, d))

    def finish(p):
        totals = []
        for a in range(2):
            total = parts[a, p, x, k] + pair[a, p, x]
            for d in range(chips - 1):
                to_chip(a, p, d).wait_recv()
                total = total + landed[a, p, d].astype(jnp.float32)
            totals.append(total)
        act, slope = gelu_parts(totals[0])
        for a, value in enumerate((act, totals[1] * slope)):
            outs[a][me, :, pl.ds(p * cols, cols)] = value.astype(outs[a].dtype)
            for d in range(chips - 1):
                push(give_chip(a, p, d, me))
            push(give_partner(a, p, chips - 1, me))

    def forward(p):
        for a in range(2):
            for d in range(chips - 1):
                owner = lax.rem(x + chips - d - 1, chips) * cores + k
                give_chip(a, p, d, owner).wait_recv()
                push(give_partner(a, p, d, owner))

    stages = (compute, reduce_pair, finish, forward)
    for step in range(pieces + len(stages) - 1):
        for lag, stage in enumerate(stages):
            if 0 <= step - lag < pieces:
                stage(step - lag)
    for p in range(pieces):
        for a in range(2):
            for d in range(chips):
                owner = lax.rem(x + chips - lax.rem(d + 1, chips), chips) * cores + (1 - k)
                give_partner(a, p, d, owner).wait_recv()
    for copy in sent:
        copy.wait_send()


ANY = pl.BlockSpec(memory_space=pl.ANY)


def row_stage(chips, cores, left, right, down, down_flags, up, up_flags):
    tokens, depth = left.shape
    width = down.shape[1]
    tile, tiles, pieces = tiling(width)
    cols = width // pieces
    share = tokens // (chips * cores)
    out = jax.ShapeDtypeStruct((chips * cores, share, width), jnp.bfloat16)
    gathered = pl.pallas_call(
        functools.partial(row_kernel, chips, cores, tile, tiles, pieces),
        out_shape=(out, out),
        in_specs=[VMEM] * 2 + [ANY] * 4,
        out_specs=(VMEM, VMEM),
        scratch_shapes=stream_shapes(depth, tile) + [
            pltpu.VMEM((2, pieces, chips, cores, share, cols), jnp.float32),
            pltpu.VMEM((2, pieces, chips, share, cols), jnp.float32),
            pltpu.VMEM((2, pieces, chips - 1, share, cols), jnp.bfloat16),
            pltpu.VMEM((2, pieces, chips - 1, share, cols), jnp.bfloat16),
            DMA((2, pieces)), DMA((2, pieces)),
            DMA((2, pieces, chips - 1)), DMA((2, pieces, chips - 1)),
            DMA((2, pieces, chips - 1)), DMA((2, pieces, chips - 1)),
            DMA((2, pieces, chips)), DMA((2, pieces, chips)),
        ],
        compiler_params=pltpu.CompilerParams(collective_id=1, has_side_effects=True),
        name="row_stage",
    )(left, right, down, down_flags, up, up_flags)
    return [each.reshape(tokens, width) for each in gathered]


def column_kernel(far, near, tile, tiles, pieces, left, right, *refs):
    sources, outs, refs = refs[:4], refs[4:6], refs[6:]
    buffers, refs = refs[:5], refs[5:]
    wide, short, across, sums, landed, ys, yr, zs, zr = refs
    me = lax.axis_index("col")
    z, y = me // near, lax.rem(me, near)
    rows_y = [lax.rem(y + e, near) for e in range(1, near)]
    rows_z = [lax.rem(z + d, far) for d in range(1, far)]
    peers_y = [z * near + e for e in rows_y]
    peers_z = [d * near + y for d in rows_z]
    first, multiply = streamed(tile, tiles, left, right, sources, buffers)
    first()
    greet("col", peers_y + peers_z)
    per = tiles // pieces
    cols = per * tile
    shaped = wide.shape[2:5]
    sent = []

    def push(copy):
        copy.start()
        sent.append(copy)

    def over_y(a, p, e):
        return remote(short.at[a, p, :, rows_y[e]], across.at[a, p, e], ys.at[a, p, e], yr.at[a, p, e], "col", peers_y[e])

    def over_z(a, p, d):
        return remote(sums.at[a, p, d], landed.at[a, p, d], zs.at[a, p, d], zr.at[a, p, d], "col", peers_z[d])

    def near_sum(a, p, row):
        total = wide[a, p, row, y]
        for e in range(near - 1):
            total = total + across[a, p, e, row].astype(jnp.float32)
        return total

    def compute(p):
        def step(j, carry):
            spot = pl.ds(pl.multiple_of(j * tile, tile), tile)
            for a, value in enumerate(multiply(p * per + j)):
                laid = value.reshape(*shaped, tile)
                wide[a, p, :, :, :, spot] = laid
                short[a, p, :, :, :, spot] = laid.astype(short.dtype)
            return carry

        lax.fori_loop(0, per, step, 0)
        for a in range(2):
            for e in range(near - 1):
                push(over_y(a, p, e))

    def reduce_near(p):
        for a in range(2):
            for e in range(near - 1):
                over_y(a, p, e).wait_recv()
            for d in range(far - 1):
                sums[a, p, d] = near_sum(a, p, rows_z[d]).astype(sums.dtype)
                push(over_z(a, p, d))

    def finish(p):
        for a in range(2):
            total = near_sum(a, p, z)
            for d in range(far - 1):
                over_z(a, p, d).wait_recv()
                total = total + landed[a, p, d].astype(jnp.float32)
            outs[a][:, pl.ds(p * cols, cols)] = total.astype(outs[a].dtype)

    stages = (compute, reduce_near, finish)
    for step in range(pieces + len(stages) - 1):
        for lag, stage in enumerate(stages):
            if 0 <= step - lag < pieces:
                stage(step - lag)
    for copy in sent:
        copy.wait_send()


def column_stage(far, near, left, right, down, down_flags, up, up_flags):
    tokens, depth = left.shape
    width = down.shape[1]
    tile, tiles, pieces = tiling(width)
    cols = width // pieces
    share = tokens // (far * near)
    out = jax.ShapeDtypeStruct((share, width), jnp.bfloat16)
    return pl.pallas_call(
        functools.partial(column_kernel, far, near, tile, tiles, pieces),
        out_shape=(out, out),
        in_specs=[VMEM] * 2 + [ANY] * 4,
        out_specs=(VMEM, VMEM),
        scratch_shapes=stream_shapes(depth, tile) + [
            pltpu.VMEM((2, pieces, far, near, share, cols), jnp.float32),
            pltpu.VMEM((2, pieces, far, near, share, cols), jnp.bfloat16),
            pltpu.VMEM((2, pieces, near - 1, far, share, cols), jnp.bfloat16),
            pltpu.VMEM((2, pieces, far - 1, share, cols), jnp.bfloat16),
            pltpu.VMEM((2, pieces, far - 1, share, cols), jnp.bfloat16),
            DMA((2, pieces, near - 1)), DMA((2, pieces, near - 1)),
            DMA((2, pieces, far - 1)), DMA((2, pieces, far - 1)),
        ],
        compiler_params=pltpu.CompilerParams(collective_id=2, has_side_effects=True),
        name="column_stage",
    )(left, right, down, down_flags, up, up_flags)


def outer_kernel(tokens_ref, hid_ref, in_flags, act_ref, grad_ref, out_flags, in_ref, out_ref):
    def one(left, right, flags, out):
        full = lax.dot_general(left, right, (((0,), (0,)), ((), ())), preferred_element_type=jnp.float32)
        out[...] = masked(full.astype(out.dtype), flags)

    one(tokens_ref[...], hid_ref[...], in_flags[...], in_ref)
    one(act_ref[...], grad_ref[...], out_flags[...], out_ref)


def outers(tokens, hid, in_flags, act, grad, out_flags):
    count, depth = tokens.shape
    width = hid.shape[1]
    steps = math.gcd(depth // BLK, width // BLK)
    steps = steps // 2 if steps % 2 == 0 else steps
    down, up = depth // steps, width // steps
    whole = lambda each: pl.BlockSpec(each.shape, lambda i: (0, 0))
    return pl.pallas_call(
        outer_kernel,
        grid=(steps,),
        out_shape=[
            jax.ShapeDtypeStruct((depth, width), jnp.bfloat16),
            jax.ShapeDtypeStruct((width, depth), jnp.bfloat16),
        ],
        in_specs=[
            pl.BlockSpec((count, down), lambda i: (0, i)), whole(hid),
            pl.BlockSpec((down // BLK * SUB, width), lambda i: (i, 0)),
            pl.BlockSpec((count, up), lambda i: (0, i)), whole(grad),
            pl.BlockSpec((up // BLK * SUB, depth), lambda i: (i, 0)),
        ],
        out_specs=[
            pl.BlockSpec((down, width), lambda i: (i, 0)),
            pl.BlockSpec((up, depth), lambda i: (i, 0)),
        ],
        name="outers",
    )(tokens, hid, in_flags, act, grad, out_flags)


def local(far, near, chips, cores, tokens, w_in, w_out, mask_in, mask_out, out_grad):
    gathered, grad_rows, in_flags, out_flags = gather(far, near, tokens, out_grad, (mask_in, mask_out))
    act, hid = row_stage(chips, cores, gathered, grad_rows, w_in, in_flags, w_out, out_flags)
    mixed, tokens_grad = column_stage(far, near, act, hid, w_out, out_flags, w_in, in_flags)
    w_in_grad, w_out_grad = outers(gathered, hid, in_flags, act, grad_rows, out_flags)
    return (mixed, tokens_grad, w_in_grad, w_out_grad)


def solution(mesh):
    columns, rows = mesh.shape["col"], mesh.shape["row"]
    near = 2 ** (int(math.log2(columns)) // 2)
    return jax.shard_map(
        functools.partial(local, columns // near, near, rows // 2, 2),
        mesh=mesh,
        in_specs=(
            P("col", "row"),
            P("row", "col"),
            P("col", "row"),
            P("row", "col"),
            P("col", "row"),
            P("col", "row"),
        ),
        out_specs=(P("col", "row"), P("col", "row"), P("row", "col"), P("col", "row")),
        check_vma=False,
    )
```

```python
import functools
import math

import jax
import jax.numpy as jnp
from jax import lax
from jax.experimental import pallas as pl
from jax.experimental.pallas import tpu as pltpu
from jax.sharding import PartitionSpec as P

BLK = 128
SUB = 16
MESH = pl.DeviceIdType.MESH
VMEM = pl.BlockSpec(memory_space=pltpu.VMEM)
DMA = pltpu.SemaphoreType.DMA
GELU_A, GELU_B = 0.7978845608028654, 0.044715


def remote(src, dst, send, recv, axis, device):
    return pltpu.make_async_remote_copy(
        src_ref=src, dst_ref=dst, send_sem=send, recv_sem=recv,
        device_id={axis: device}, device_id_type=MESH,
    )


def greet(axis, peers):
    barrier = pltpu.get_barrier_semaphore()
    for peer in peers:
        pl.semaphore_signal(barrier, inc=1, device_id={axis: peer}, device_id_type=MESH)
    pl.semaphore_wait(barrier, len(peers))


def spread(mask):
    rows, cols = mask.shape

    def repeats(shape, dim, size):
        apart = lax.broadcasted_iota(jnp.int32, shape, dim) - size * lax.broadcasted_iota(jnp.int32, shape, 1 - dim)
        return jnp.where((apart >= 0) & (apart < size), 1.0, 0.0).astype(jnp.bfloat16)

    flags = mask.astype(jnp.float32).astype(jnp.bfloat16)
    tall = jnp.dot(repeats((rows * SUB, rows), 0, SUB), flags, preferred_element_type=jnp.float32)
    wide = jnp.dot(tall.astype(jnp.bfloat16), repeats((cols, cols * BLK), 1, BLK), preferred_element_type=jnp.float32)
    return wide.astype(jnp.bfloat16)


def masked(weight, flags):
    rows, cols = weight.shape
    shaped = weight.reshape(rows // BLK, BLK // SUB, SUB, cols)
    return (shaped * flags.reshape(rows // BLK, 1, SUB, cols)).reshape(rows, cols)


def tiling(width):
    tile = 2 * BLK if width % (2 * BLK) == 0 else BLK
    tiles = width // tile
    pieces = next(count for count in (4, 3, 2, 1) if tiles % count == 0)
    return tile, tiles, pieces


def stream_shapes(depth, tile):
    return [
        pltpu.VMEM((2, depth, tile), jnp.bfloat16), pltpu.VMEM((2, depth // BLK * SUB, tile), jnp.bfloat16),
        pltpu.VMEM((2, tile, depth), jnp.bfloat16), pltpu.VMEM((2, tile // BLK * SUB, depth), jnp.bfloat16),
        DMA((4, 2)),
    ]


def streamed(tile, tiles, left, right, sources, buffers):
    *slots, arrived = buffers
    rows = tile // BLK * SUB

    def copies(t):
        slot = lax.rem(t, 2)
        across = pl.ds(pl.multiple_of(t * tile, tile), tile)
        down = pl.ds(pl.multiple_of(t * rows, rows), rows)
        views = [sources[0].at[:, across], sources[1].at[:, across], sources[2].at[across, :], sources[3].at[down, :]]
        return [pltpu.make_async_copy(view, slots[n].at[slot], arrived.at[n, slot]) for n, view in enumerate(views)]

    def first():
        for copy in copies(0):
            copy.start()

    def pair(t):
        for copy in copies(t):
            copy.wait()

        @pl.when(t + 1 < tiles)
        def _():
            for copy in copies(t + 1):
                copy.start()

        slot = lax.rem(t, 2)
        ahead = jnp.dot(left[...], masked(slots[0][slot], slots[1][slot]), preferred_element_type=jnp.float32)
        back = lax.dot_general(
            right[...], masked(slots[2][slot], slots[3][slot]),
            (((1,), (1,)), ((), ())), preferred_element_type=jnp.float32,
        )
        return ahead, back

    return first, pair


def gelu_parts(value):
    square = value * value
    tanh = jnp.tanh(GELU_A * (value + GELU_B * (square * value)))
    half = 0.5 * (1.0 + tanh)
    slope = half + 0.5 * value * (1.0 - tanh * tanh) * (GELU_A * (1.0 + (3.0 * GELU_B) * square))
    return value * half, slope


def front_kernel(far, near, chips, cores, tile, tiles, pieces, *refs):
    srcs, masks, weights, outs, dsts, flags = (refs[n:n + 2] for n in range(0, 12, 2))
    down_slots, up_slots, arrived, zs, zr, ys, yr, own = refs[12:20]
    parts, pair, sums, landed, slopes, ps, pr, xs, xr, gs, gr, fs, fr = refs[20:]
    slots = (down_slots, up_slots)
    mine = lax.axis_index("col")
    z, y = mine // near, lax.rem(mine, near)
    along_z = [lax.rem(z + d, far) * near + y for d in range(1, far)]
    along_y = [z * near + lax.rem(y + e, near) for e in range(1, near)]
    me = lax.axis_index("row")
    x, k = me // cores, lax.rem(me, cores)
    partner = x * cores + (1 - k)
    across = [lax.rem(x + d, chips) for d in range(1, chips)]
    peers = [c * cores + k for c in across]
    per = tiles // pieces
    cols = per * tile
    shaped = parts.shape[2:5]
    rows = tile // BLK * SUB
    sent = []

    def push(copy):
        copy.start()
        sent.append(copy)

    def fetch(a, t):
        slot = lax.rem(t, 2)
        spot = pl.ds(pl.multiple_of(t * tile, tile), tile)
        view = weights[0].at[:, spot] if a == 0 else weights[1].at[spot, :]
        return pltpu.make_async_copy(view, slots[a].at[slot], arrived.at[a, slot])

    for a in range(2):
        fetch(a, jnp.int32(0)).start()
    barrier = pltpu.get_barrier_semaphore()
    for axis, group in (("col", along_z + along_y), ("row", [partner] + peers)):
        for peer in group:
            pl.semaphore_signal(barrier, inc=1, device_id={axis: peer}, device_id_type=MESH)
    pl.semaphore_wait(barrier, len(along_z) + len(along_y) + len(peers) + 1)

    for a in range(2):
        for e, peer in enumerate(along_y):
            push(remote(srcs[a], dsts[a].at[mine], ys.at[a, 0, e], yr.at[a, 0, e], "col", peer))
        for d, peer in enumerate(along_z):
            push(remote(srcs[a], dsts[a].at[mine], zs.at[a, d], zr.at[a, d], "col", peer))
    kept = [pltpu.make_async_copy(srcs[a], dsts[a].at[mine], own.at[a]) for a in range(2)]
    for copy in kept:
        copy.start()
    for a in range(2):
        flags[a][...] = spread(masks[a][...])

    def relay(a, d):
        slot = dsts[a].at[lax.rem(z + far - d - 1, far) * near + y]
        remote(srcs[a], slot, zs.at[a, d], zr.at[a, d], "col", along_z[d]).wait_recv()
        for e, peer in enumerate(along_y):
            push(remote(slot, slot, ys.at[a, d + 1, e], yr.at[a, d + 1, e], "col", peer))

    def gathered(a):
        for d in range(far):
            for e in range(near - 1):
                slot = dsts[a].at[lax.rem(z + far - d, far) * near + lax.rem(y + near - e - 1, near)]
                remote(slot, slot, ys.at[a, d, e], yr.at[a, d, e], "col", along_y[e]).wait_recv()
        kept[a].wait()

    def to_partner(a, p):
        return remote(parts.at[a, p, :, 1 - k], pair.at[a, p], ps.at[a, p], pr.at[a, p], "row", partner)

    def to_chip(a, p, d):
        return remote(sums.at[a, p, d], landed.at[a, p, d], xs.at[a, p, d], xr.at[a, p, d], "row", peers[d])

    def share(a, p, owner):
        return outs[a].at[owner, :, pl.ds(p * cols, cols)]

    def give_chip(a, p, d, owner):
        return remote(share(a, p, owner), share(a, p, owner), gs.at[a, p, d], gr.at[a, p, d], "row", peers[d])

    def give_partner(a, p, d, owner):
        return remote(share(a, p, owner), share(a, p, owner), fs.at[a, p, d], fr.at[a, p, d], "row", partner)

    def compute(a, p):
        if p == 0:
            gathered(a)

        def step(j, carry):
            t = p * per + j
            slot = lax.rem(t, 2)
            fetch(a, t).wait()

            @pl.when(t + 1 < tiles)
            def _():
                fetch(a, t + 1).start()

            left = dsts[a][...].reshape(-1, dsts[a].shape[-1])
            if a == 0:
                marks = flags[0][:, pl.ds(pl.multiple_of(t * tile, tile), tile)]
            else:
                marks = flags[1][pl.ds(pl.multiple_of(t * rows, rows), rows), :]
            value = lax.dot_general(
                left, masked(slots[a][slot], marks), (((1,), (a,)), ((), ())), preferred_element_type=jnp.float32
            )
            parts[a, p, :, :, :, pl.ds(pl.multiple_of(j * tile, tile), tile)] = value.reshape(*shaped, tile)
            return carry

        lax.fori_loop(0, per, step, 0)
        push(to_partner(a, p))
        if a == 0:
            for d in range(far - 1):
                if d * pieces // (far - 1) == p:
                    relay(1, d)

    def reduce_pair(a, p):
        to_partner(a, p).wait_recv()
        for d, c in enumerate(across):
            sums[a, p, d] = (parts[a, p, c, k] + pair[a, p, c]).astype(sums.dtype)
            push(to_chip(a, p, d))

    def finish(a, p):
        total = parts[a, p, x, k] + pair[a, p, x]
        for d in range(chips - 1):
            to_chip(a, p, d).wait_recv()
            total = total + landed[a, p, d].astype(jnp.float32)
        if a == 0:
            value, slopes[p] = gelu_parts(total)
        else:
            value = total * slopes[p]
        outs[a][me, :, pl.ds(p * cols, cols)] = value.astype(outs[a].dtype)
        for d in range(chips - 1):
            push(give_chip(a, p, d, me))
        push(give_partner(a, p, chips - 1, me))

    def forward(a, p):
        for d in range(chips - 1):
            owner = lax.rem(x + chips - d - 1, chips) * cores + k
            give_chip(a, p, d, owner).wait_recv()
            push(give_partner(a, p, d, owner))

    for d in range(far - 1):
        relay(0, d)
    stages = (compute, reduce_pair, finish, forward)
    jobs = [(a, p) for a in range(2) for p in range(pieces)]
    for step in range(len(jobs) + len(stages) - 1):
        for lag, stage in enumerate(stages):
            if 0 <= step - lag < len(jobs):
                stage(*jobs[step - lag])
    for a, p in jobs:
        for d in range(chips):
            owner = lax.rem(x + chips - lax.rem(d + 1, chips), chips) * cores + (1 - k)
            give_partner(a, p, d, owner).wait_recv()
    for copy in sent:
        copy.wait_send()


ANY = pl.BlockSpec(memory_space=pl.ANY)


def front_stage(far, near, chips, cores, first, second, masks, down, up):
    depth, width = down.shape
    tokens = first.shape[0] * far * near
    tile, tiles, pieces = tiling(width)
    cols = width // pieces
    share = tokens // (chips * cores)
    out = jax.ShapeDtypeStruct((chips * cores, share, width), jnp.bfloat16)
    full = jax.ShapeDtypeStruct((far * near,) + first.shape, first.dtype)
    spreads = tuple(
        jax.ShapeDtypeStruct((each.shape[0] * SUB, each.shape[1] * BLK), jnp.bfloat16) for each in masks
    )
    act, hid, gathered, grad_rows, in_flags, out_flags = pl.pallas_call(
        functools.partial(front_kernel, far, near, chips, cores, tile, tiles, pieces),
        out_shape=(out, out, full, full) + spreads,
        in_specs=[VMEM] * 4 + [ANY] * 2,
        out_specs=(VMEM,) * 6,
        scratch_shapes=[
            pltpu.VMEM((2, depth, tile), jnp.bfloat16), pltpu.VMEM((2, tile, depth), jnp.bfloat16), DMA((2, 2)),
            DMA((2, far - 1)), DMA((2, far - 1)),
            DMA((2, far, near - 1)), DMA((2, far, near - 1)), DMA((2,)),
            pltpu.VMEM((2, pieces, chips, cores, share, cols), jnp.float32),
            pltpu.VMEM((2, pieces, chips, share, cols), jnp.float32),
            pltpu.VMEM((2, pieces, chips - 1, share, cols), jnp.bfloat16),
            pltpu.VMEM((2, pieces, chips - 1, share, cols), jnp.bfloat16),
            pltpu.VMEM((pieces, share, cols), jnp.float32),
            DMA((2, pieces)), DMA((2, pieces)),
            DMA((2, pieces, chips - 1)), DMA((2, pieces, chips - 1)),
            DMA((2, pieces, chips - 1)), DMA((2, pieces, chips - 1)),
            DMA((2, pieces, chips)), DMA((2, pieces, chips)),
        ],
        compiler_params=pltpu.CompilerParams(collective_id=0, has_side_effects=True),
        name="front_stage",
    )(first, second, *masks, down, up)
    flat = lambda each: each.reshape(tokens, each.shape[-1])
    return flat(act), flat(hid), flat(gathered), flat(grad_rows), in_flags, out_flags


def column_kernel(far, near, tile, tiles, pieces, left, right, *refs):
    sources, outs, refs = refs[:4], refs[4:6], refs[6:]
    buffers, refs = refs[:5], refs[5:]
    wide, short, across, sums, landed, ys, yr, zs, zr = refs
    me = lax.axis_index("col")
    z, y = me // near, lax.rem(me, near)
    rows_y = [lax.rem(y + e, near) for e in range(1, near)]
    rows_z = [lax.rem(z + d, far) for d in range(1, far)]
    peers_y = [z * near + e for e in rows_y]
    peers_z = [d * near + y for d in rows_z]
    first, multiply = streamed(tile, tiles, left, right, sources, buffers)
    first()
    greet("col", peers_y + peers_z)
    per = tiles // pieces
    cols = per * tile
    shaped = wide.shape[2:5]
    sent = []

    def push(copy):
        copy.start()
        sent.append(copy)

    def over_y(a, p, e):
        return remote(short.at[a, p, :, rows_y[e]], across.at[a, p, e], ys.at[a, p, e], yr.at[a, p, e], "col", peers_y[e])

    def over_z(a, p, d):
        return remote(sums.at[a, p, d], landed.at[a, p, d], zs.at[a, p, d], zr.at[a, p, d], "col", peers_z[d])

    def near_sum(a, p, row):
        total = wide[a, p, row, y]
        for e in range(near - 1):
            total = total + across[a, p, e, row].astype(jnp.float32)
        return total

    def compute(p):
        def step(j, carry):
            spot = pl.ds(pl.multiple_of(j * tile, tile), tile)
            for a, value in enumerate(multiply(p * per + j)):
                laid = value.reshape(*shaped, tile)
                wide[a, p, :, :, :, spot] = laid
                short[a, p, :, :, :, spot] = laid.astype(short.dtype)
            return carry

        lax.fori_loop(0, per, step, 0)
        for a in range(2):
            for e in range(near - 1):
                push(over_y(a, p, e))

    def reduce_near(p):
        for a in range(2):
            for e in range(near - 1):
                over_y(a, p, e).wait_recv()
            for d in range(far - 1):
                sums[a, p, d] = near_sum(a, p, rows_z[d]).astype(sums.dtype)
                push(over_z(a, p, d))

    def finish(p):
        for a in range(2):
            total = near_sum(a, p, z)
            for d in range(far - 1):
                over_z(a, p, d).wait_recv()
                total = total + landed[a, p, d].astype(jnp.float32)
            outs[a][:, pl.ds(p * cols, cols)] = total.astype(outs[a].dtype)

    stages = (compute, reduce_near, finish)
    for step in range(pieces + len(stages) - 1):
        for lag, stage in enumerate(stages):
            if 0 <= step - lag < pieces:
                stage(step - lag)
    for copy in sent:
        copy.wait_send()


def column_stage(far, near, left, right, down, down_flags, up, up_flags):
    tokens, depth = left.shape
    width = down.shape[1]
    tile, tiles, pieces = tiling(width)
    cols = width // pieces
    share = tokens // (far * near)
    out = jax.ShapeDtypeStruct((share, width), jnp.bfloat16)
    return pl.pallas_call(
        functools.partial(column_kernel, far, near, tile, tiles, pieces),
        out_shape=(out, out),
        in_specs=[VMEM] * 2 + [ANY] * 4,
        out_specs=(VMEM, VMEM),
        scratch_shapes=stream_shapes(depth, tile) + [
            pltpu.VMEM((2, pieces, far, near, share, cols), jnp.float32),
            pltpu.VMEM((2, pieces, far, near, share, cols), jnp.bfloat16),
            pltpu.VMEM((2, pieces, near - 1, far, share, cols), jnp.bfloat16),
            pltpu.VMEM((2, pieces, far - 1, share, cols), jnp.bfloat16),
            pltpu.VMEM((2, pieces, far - 1, share, cols), jnp.bfloat16),
            DMA((2, pieces, near - 1)), DMA((2, pieces, near - 1)),
            DMA((2, pieces, far - 1)), DMA((2, pieces, far - 1)),
        ],
        compiler_params=pltpu.CompilerParams(collective_id=2, has_side_effects=True),
        name="column_stage",
    )(left, right, down, down_flags, up, up_flags)


def outer_kernel(tokens_ref, hid_ref, in_flags, act_ref, grad_ref, out_flags, in_ref, out_ref):
    def one(left, right, flags, out):
        full = lax.dot_general(left, right, (((0,), (0,)), ((), ())), preferred_element_type=jnp.float32)
        out[...] = masked(full.astype(out.dtype), flags)

    one(tokens_ref[...], hid_ref[...], in_flags[...], in_ref)
    one(act_ref[...], grad_ref[...], out_flags[...], out_ref)


def outers(tokens, hid, in_flags, act, grad, out_flags):
    count, depth = tokens.shape
    width = hid.shape[1]
    steps = math.gcd(depth // BLK, width // BLK)
    steps = steps // 2 if steps % 2 == 0 else steps
    down, up = depth // steps, width // steps
    whole = lambda each: pl.BlockSpec(each.shape, lambda i: (0, 0))
    return pl.pallas_call(
        outer_kernel,
        grid=(steps,),
        out_shape=[
            jax.ShapeDtypeStruct((depth, width), jnp.bfloat16),
            jax.ShapeDtypeStruct((width, depth), jnp.bfloat16),
        ],
        in_specs=[
            pl.BlockSpec((count, down), lambda i: (0, i)), whole(hid),
            pl.BlockSpec((down // BLK * SUB, width), lambda i: (i, 0)),
            pl.BlockSpec((count, up), lambda i: (0, i)), whole(grad),
            pl.BlockSpec((up // BLK * SUB, depth), lambda i: (i, 0)),
        ],
        out_specs=[
            pl.BlockSpec((down, width), lambda i: (i, 0)),
            pl.BlockSpec((up, depth), lambda i: (i, 0)),
        ],
        name="outers",
    )(tokens, hid, in_flags, act, grad, out_flags)


def local(far, near, chips, cores, tokens, w_in, w_out, mask_in, mask_out, out_grad):
    act, hid, gathered, grad_rows, in_flags, out_flags = front_stage(
        far, near, chips, cores, tokens, out_grad, (mask_in, mask_out), w_in, w_out
    )
    mixed, tokens_grad = column_stage(far, near, act, hid, w_out, out_flags, w_in, in_flags)
    w_in_grad, w_out_grad = outers(gathered, hid, in_flags, act, grad_rows, out_flags)
    return (mixed, tokens_grad, w_in_grad, w_out_grad)


def solution(mesh):
    columns, rows = mesh.shape["col"], mesh.shape["row"]
    near = 2 ** (int(math.log2(columns)) // 2)
    return jax.shard_map(
        functools.partial(local, columns // near, near, rows // 2, 2),
        mesh=mesh,
        in_specs=(
            P("col", "row"),
            P("row", "col"),
            P("col", "row"),
            P("row", "col"),
            P("col", "row"),
            P("col", "row"),
        ),
        out_specs=(P("col", "row"), P("col", "row"), P("row", "col"), P("col", "row")),
        check_vma=False,
    )
```
